32 devices in a mesh: expert: 8 (over z, y), dp: 4 (over x, core).
Axes of the slice: x: 2, y: 2, z: 4, core: 2. Of those that a mesh axis runs over, the one named last changes fastest.
Arguments:
- tokens: bfloat16 [4096, 3584], P(('expert', 'dp')), may hold values from -6 to 6
- cotangent: bfloat16 [4096, 3584], P(('expert', 'dp')), may hold values from -6 to 6
- routes: int32 [4096, 1], P(('expert', 'dp')), may hold values from 0 to 1; in each aligned block of 128 rows (0 to 127, 128 to 255, ...) at most 80 rows name the same one
- gates: bfloat16 [4096, 1], P(('expert', 'dp')), may hold values from 0.049804688 to 1
- w_gate: bfloat16 [2048, 3584], P('expert', 'dp'), may hold values from -0.09375 to 0.09375
- w_up: bfloat16 [2048, 3584], P('expert', 'dp'), may hold values from -0.09375 to 0.09375
- w_down: bfloat16 [2048, 3584], P('expert', 'dp'), may hold values from -0.1875 to 0.1875
Outputs:
- grad_up: bfloat16 [2048, 3584], P('expert', 'dp')
- grad_down: bfloat16 [2048, 3584], P('expert', 'dp')
- grad_gates: float32 [4096, 1], P(('expert', 'dp'))
The draws below stay inside these ranges and needn't reach their ends.
Inputs may be any that keep to these rules, and one draw needn't show every extreme that they name: `routes`: the 1 entries of a row are distinct. Among the 128 rows of one device, no expert is named more than 80 times, a bound that some block reaches.
All inputs are finite; a program needn't handle non-finite values.
Results may differ from the reference program's by a relative error of at most 0.009.
Values may be sent and summed in bfloat16 or wider, within the bound.
A program may use at most 128 MiB of HBM per device.

```python
import math
import jax
import jax.numpy as jnp
import numpy as np
from jax import lax

D = 3584
FF = 1024
TOP = 1
TOK_DEV = 128
EXPERTS = 2
CAP = 80
TOKENS = 4096
N_EXPERT = 8
N_DP = 4


def block_scale(own_key, shape, split, low, top_value):
    loudness = 1.0
    for axis_at, blocks in split:
        heights = jax.random.uniform(jax.random.fold_in(jax.random.fold_in(own_key, 6), axis_at), (blocks,), jnp.float32, low / len(split), top_value / len(split))
        loudness = loudness * jnp.repeat(jnp.exp(heights), shape[axis_at] // blocks).reshape((-1,) + (1,) * (len(shape) - 1 - axis_at))
    return loudness


def deal_out(stream_key, own, number, rows, count, top, most, slope):
    order = jax.random.permutation(stream_key, count)
    crowded, usual = load_shares(count, rows * top, most, slope, True), load_shares(count, rows * top, most, slope, False)
    places = jnp.arange(count)

    def named(sizes, offset_by):
        used = int((sizes > 0).sum())
        fixed = max(1, used // 4)
        moved = fixed + (places - fixed + offset_by * (used - fixed)) % max(1, count - fixed)
        return jnp.zeros((count,), jnp.int32).at[order[jnp.where(places < fixed, places, moved)]].set(jnp.asarray(sizes, jnp.int32))

    sizes = jnp.where(number % 4 == 0, named(crowded, number // 4), named(usual, number - number // 4 - 1))
    mixed = jax.random.permutation(jax.random.fold_in(own, 3), count)
    donor, receiver = mixed[0:count // 2 * 2:2], mixed[1:count // 2 * 2:2]
    slack = jnp.minimum(sizes[donor] - 1, most - sizes[receiver]) // 2
    slack = jnp.where((donor == order[0]) | (receiver == order[0]) | (sizes[receiver] == 0), 0, jnp.maximum(slack, 0))
    moved = jax.random.randint(jax.random.fold_in(own, 4), (count // 2,), 0, 1 << 20) % (slack + 1)
    sizes = sizes.at[donor].add(-moved).at[receiver].add(moved)
    items = jnp.searchsorted(jnp.cumsum(sizes), jnp.arange(rows * top), side="right").astype(jnp.int32)
    listing = items.reshape(top, rows).T
    listing = listing[jax.random.permutation(jax.random.fold_in(own, 1), rows)]
    offset_by = jax.random.randint(jax.random.fold_in(own, 2), (rows, 1), 0, top)
    return jnp.take_along_axis(listing, (jnp.arange(top)[None, :] + offset_by) % top, axis=1)


def load_shares(amount, total, reach, slope, full):
    portions = [(1 << 20) // math.isqrt(grade ** slope) + 1 for grade in range(1, amount + 1)]
    largest = reach if full else min(reach, max(-(-total // amount), total * portions[0] // sum(portions)))
    least = 1 if total - largest >= amount - 1 else 0
    counts, rest = [largest] + [least] * (amount - 1), total - largest - least * (amount - 1)
    while rest > 0:
        candidates = [i for i in range(1, amount) if counts[i] < largest] or [i for i in range(1, amount) if counts[i] < reach]
        pool, remaining = sum([portions[i] for i in candidates]), rest
        for i in candidates:
            addition = min(reach - counts[i], max(1, remaining * portions[i] // pool), rest)
            counts[i] = counts[i] + addition
            rest = rest - addition
    return np.array(counts)


def bell_draw(own_key, extent, deviation, bound, split=(), kind=jnp.bfloat16):
    values = jax.random.normal(own_key, extent, jnp.float32) * deviation
    if len(split) > 0:
        values = block_scale(own_key, extent, split, -0.22, 0.18) * values
    return jnp.clip(values, min=-bound, max=bound).astype(kind)


def setup_inputs(seed: int = 0) -> dict:
    arg_keys = jax.random.split(jax.random.key(seed), 8)
    tokens = bell_draw(arg_keys[0], (TOKENS, D), 1.0, 6.0, ((0, 32),))
    cotangent = bell_draw(arg_keys[1], (TOKENS, D), 1.0, 6.0, ((0, 32),))
    routes_keys = jax.random.split(jax.random.fold_in(arg_keys[2], 1), TOKENS // TOK_DEV)
    routes_turns = jax.random.permutation(jax.random.fold_in(arg_keys[2], 3), TOKENS // TOK_DEV)
    routes = jax.vmap(lambda own, number: deal_out(jax.random.fold_in(arg_keys[2], 2), own, number, TOK_DEV, EXPERTS, TOP, CAP, 1))(routes_keys, routes_turns).reshape((TOKENS, TOP))
    gates = jnp.clip(jnp.exp(math.log(1.0) - 2.9996462 * jax.random.uniform(arg_keys[3], (TOKENS, TOP), jnp.float32) ** block_scale(arg_keys[3], (TOKENS, TOP), ((0, 32),), -0.2, 0.2)), 0.049804688, 1.0).astype(jnp.bfloat16)
    w_gate = bell_draw(arg_keys[4], (EXPERTS * FF, D), D ** -0.5, 0.09375, ((0, 8), (1, 4)))
    w_up = bell_draw(arg_keys[5], (EXPERTS * FF, D), D ** -0.5, 0.09375, ((0, 8), (1, 4)))
    w_down = bell_draw(arg_keys[6], (EXPERTS * FF, D), FF ** -0.5, 0.1875, ((0, 8), (1, 4)))
    return dict(tokens=tokens, cotangent=cotangent, routes=routes, gates=gates, w_gate=w_gate, w_up=w_up, w_down=w_down)


def reference(tokens, cotangent, routes, gates, w_gate, w_up, w_down):
    total = tokens.shape[0]
    experts = w_gate.shape[0] // FF
    pairs = total * TOP
    limit = N_DP * N_EXPERT * CAP
    flat_routes = routes.reshape(-1)
    flat_gates = gates.reshape(-1)

    def one_expert(expert_id):
        mask = flat_routes == expert_id
        order = jnp.cumsum(mask.astype(jnp.int32)) - 1
        target = jnp.where(mask, order, limit).astype(jnp.int32)
        picked = jnp.zeros((limit,), jnp.int32).at[target].set(jnp.arange(pairs, dtype=jnp.int32), mode="drop")
        count = jnp.sum(mask.astype(jnp.int32))
        valid = jnp.arange(limit, dtype=jnp.int32) < count
        tok_index = picked // TOP
        rows_x = jnp.where(valid[:, None], tokens[tok_index], jnp.zeros((), jnp.bfloat16))
        rows_dy = jnp.where(valid[:, None], cotangent[tok_index], jnp.zeros((), jnp.bfloat16))
        weight = jnp.where(valid, flat_gates[picked].astype(jnp.float32), jnp.float32(0.0))
        start = (expert_id * FF).astype(jnp.int32)
        wg = lax.dynamic_slice_in_dim(w_gate, start, FF, 0)
        wu = lax.dynamic_slice_in_dim(w_up, start, FF, 0)
        wd = lax.dynamic_slice_in_dim(w_down, start, FF, 0)
        pre_a = jnp.dot(rows_x, wg.T, preferred_element_type=jnp.float32)
        pre_b = jnp.dot(rows_x, wu.T, preferred_element_type=jnp.float32)
        sig = jax.nn.sigmoid(pre_a)
        silu = pre_a * sig
        hidden = (silu * pre_b).astype(jnp.bfloat16)
        probe = jnp.dot(rows_dy, wd.T, preferred_element_type=jnp.float32)
        gate_grad = jnp.sum(hidden.astype(jnp.float32) * probe, axis=1)
        scaled = (weight[:, None] * rows_dy.astype(jnp.float32)).astype(jnp.bfloat16)
        d_b = (weight[:, None] * probe * silu).astype(jnp.bfloat16)
        replica = (tok_index // TOK_DEV) % N_DP
        sum_up = jnp.zeros((FF, D), jnp.float32)
        sum_down = jnp.zeros((FF, D), jnp.float32)
        zero_b = jnp.zeros((), jnp.bfloat16)
        for rep in range(N_DP):
            select = (valid & (replica == rep))[:, None]
            part_b = jnp.where(select, d_b, zero_b)
            part_h = jnp.where(select, hidden, zero_b)
            sum_up = sum_up + jnp.dot(part_b.T, rows_x, preferred_element_type=jnp.float32).astype(jnp.bfloat16).astype(jnp.float32)
            sum_down = sum_down + jnp.dot(part_h.T, scaled, preferred_element_type=jnp.float32).astype(jnp.bfloat16).astype(jnp.float32)
        where_back = jnp.where(valid, picked, pairs).astype(jnp.int32)
        return (sum_up.astype(jnp.bfloat16), sum_down.astype(jnp.bfloat16), gate_grad, where_back)

    grad_u, grad_d, gate_rows, where_all = lax.map(one_expert, jnp.arange(experts, dtype=jnp.int32))
    flat_grad = jnp.zeros((pairs,), jnp.float32).at[where_all.reshape(-1)].add(gate_rows.reshape(-1), mode="drop")
    return (grad_u.reshape(experts * FF, D), grad_d.reshape(experts * FF, D), flat_grad.reshape(total, TOP))
```

```python
import jax
import jax.numpy as jnp
from jax import lax
from jax.experimental import pallas as pl
from jax.experimental.pallas import tpu as pltpu
from jax.sharding import PartitionSpec as P

SPLIT = 4
TOP = 1
TOK_DEV = 128
MESH = pl.DeviceIdType.MESH
ORDER = (0, 4, 2, 1, 5, 6, 3, 7)
PLACE = tuple(ORDER.index(c) for c in range(8))


def flip(index, code):
    for bit in (1, 2, 4):
        if code & bit:
            index = index + bit - 2 * bit * ((index // bit) % 2)
    return index


def fused_kernel(
    cap, oh_ref, ohg_ref, tok_ref, cot_ref, wg_ref, wu_ref, wd_ref,
    up_ref, down_ref, share_ref,
    rows_x, rows_c, far_x, far_c, w_all, t_a, t_b, t_p, t_h, t_d, part, from_core, from_x, to_x,
    share_mine, share_all, local_sem,
    row_send, row_recv, w_send, w_recv, core_send, core_recv, x_send, x_recv, share_send, share_recv,
):
    e = lax.axis_index("expert")
    d = lax.axis_index("dp")
    cols = wg_ref.shape[1]
    nt = (((1,), (1,)), ((), ()))
    nn = (((1,), (0,)), ((), ()))
    f32, bf16 = jnp.float32, jnp.bfloat16

    barrier = pltpu.get_barrier_semaphore()
    for code in range(1, 8):
        pl.semaphore_signal(barrier, inc=1, device_id={"expert": flip(e, code)}, device_id_type=MESH)
    for code in (1, 2):
        pl.semaphore_signal(barrier, inc=1, device_id={"dp": flip(d, code)}, device_id_type=MESH)
    pl.semaphore_wait(barrier, 9)

    sent = []

    def band(index):
        return pl.ds(pl.multiple_of(index * cols, 128), cols)

    w_in = (wg_ref, wu_ref, wd_ref)
    w_copy = {}
    local = []
    for k in range(3):
        for code in (2, 1):
            copy = pltpu.make_async_remote_copy(
                src_ref=w_in[k], dst_ref=w_all.at[k, :, band(d)],
                send_sem=w_send.at[k, code - 1], recv_sem=w_recv.at[k, code - 1],
                device_id={"dp": flip(d, code)}, device_id_type=MESH,
            )
            copy.start()
            sent.append(copy)
            w_copy[k, code] = copy
        here = pltpu.make_async_copy(w_in[k], w_all.at[k, :, band(d)], local_sem.at[k])
        here.start()
        local.append(here)

    def at(ref, code):
        return ref.at[pl.ds(PLACE[code] * cap, cap), :]

    rows = (rows_x, rows_c)
    row_copy = {}

    def send_row(kind, slot, hop, source=None):
        there = slot ^ hop
        copy = pltpu.make_async_remote_copy(
            src_ref=at(rows[kind], slot) if source is None else source,
            dst_ref=at(rows[kind], there),
            send_sem=row_send.at[kind, there], recv_sem=row_recv.at[kind, there],
            device_id={"expert": flip(e, hop)}, device_id_type=MESH,
        )
        copy.start()
        sent.append(copy)
        row_copy[kind, there] = copy

    def pick(hot, source):
        return lax.dot_general(hot, source, nn, preferred_element_type=f32).astype(bf16)

    for kind, hot, source, far in ((0, oh_ref, tok_ref, far_x), (1, ohg_ref, cot_ref, far_c)):
        far[...] = pick(hot[cap:, :], source[...])
        send_row(kind, 0, 4, far)
        at(rows[kind], 0)[...] = pick(hot[:cap, :], source[...])
        send_row(kind, 0, 2)
        send_row(kind, 0, 1)

    def got(kind, code):
        row_copy[kind, code].wait_recv()

    def project(dst, k, kind, low, high):
        dst[:, low:high] = lax.dot_general(
            w_all[k], rows[kind][low:high, :], nt, preferred_element_type=f32
        )

    def gated(low, high):
        a = t_a[:, low:high]
        p = t_p[:, low:high]
        silu = a * jax.nn.sigmoid(a)
        h = (silu * t_b[:, low:high]).astype(bf16)
        t_h[:, low:high] = h
        t_d[:, low:high] = (p * silu).astype(bf16)
        total = jnp.sum(h.astype(f32) * p, axis=0, keepdims=True)
        share_mine[:, low:high] = jnp.broadcast_to(total, (8, high - low))

    got(0, 4)
    send_row(0, 4, 2)
    send_row(0, 4, 1)
    got(0, 2)
    send_row(0, 2, 1)
    got(1, 4)
    send_row(1, 4, 2)
    send_row(1, 4, 1)
    for k in range(3):
        w_copy[k, 2].wait_recv()
        relay = pltpu.make_async_remote_copy(
            src_ref=w_all.at[k, :, band(flip(d, 2))], dst_ref=w_all.at[k, :, band(flip(d, 2))],
            send_sem=w_send.at[k, 2], recv_sem=w_recv.at[k, 2],
            device_id={"dp": flip(d, 1)}, device_id_type=MESH,
        )
        relay.start()
        sent.append(relay)
        w_copy[k, 3] = relay
    got(1, 2)
    send_row(1, 2, 1)
    got(0, 1)
    for k in range(3):
        local[k].wait()
        w_copy[k, 1].wait_recv()
        w_copy[k, 3].wait_recv()
    project(t_a, 0, 0, 0, 256)
    got(0, 6)
    send_row(0, 6, 1)
    got(1, 5)
    send_row(1, 5, 2)
    project(t_b, 1, 0, 0, 256)
    got(1, 1)
    project(t_p, 2, 1, 0, 256)
    gated(0, 256)
    got(0, 5)
    got(0, 3)
    project(t_a, 0, 0, 256, 512)
    project(t_b, 1, 0, 256, 512)
    got(1, 6)
    got(1, 3)
    project(t_p, 2, 1, 256, 512)
    gated(256, 512)
    count = rows_x.shape[0]
    got(0, 7)
    project(t_a, 0, 0, 512, count)
    project(t_b, 1, 0, 512, count)
    got(1, 7)
    project(t_p, 2, 1, 512, count)
    gated(512, count)

    share_copy = []
    for code in range(1, 8):
        copy = pltpu.make_async_remote_copy(
            src_ref=share_mine, dst_ref=share_all.at[code],
            send_sem=share_send.at[code], recv_sem=share_recv.at[code],
            device_id={"expert": flip(e, code)}, device_id_type=MESH,
        )
        copy.start()
        sent.append(copy)
        share_copy.append(copy)

    left = (t_d, t_h)
    right = (rows_x, rows_c)

    def block(g, code):
        part[g, code] = lax.dot_general(
            left[g][...], right[g][:, band(flip(d, code))], nn, preferred_element_type=f32
        ).astype(bf16)

    core_copy = {}
    x_copy = {}

    def to_core(g, code):
        block(g, code)
        copy = pltpu.make_async_remote_copy(
            src_ref=part.at[g, code], dst_ref=from_core.at[g, code // 2],
            send_sem=core_send.at[g, code // 2], recv_sem=core_recv.at[g, code // 2],
            device_id={"dp": flip(d, 1)}, device_id_type=MESH,
        )
        copy.start()
        sent.append(copy)
        core_copy[g, code // 2] = copy

    for g in (1, 0):
        to_core(g, 3)
        block(g, 2)
        core_copy[g, 1].wait_recv()
        to_x[g] = (part[g, 2].astype(f32) + from_core[g, 1].astype(f32)).astype(bf16)
        copy = pltpu.make_async_remote_copy(
            src_ref=to_x.at[g], dst_ref=from_x.at[g],
            send_sem=x_send.at[g], recv_sem=x_recv.at[g],
            device_id={"dp": flip(d, 2)}, device_id_type=MESH,
        )
        copy.start()
        sent.append(copy)
        x_copy[g] = copy
    for g in (1, 0):
        to_core(g, 1)
        block(g, 0)
    share_ref[0:1, :] = share_mine[0:1, :]
    for code in range(1, 8):
        share_copy[code - 1].wait_recv()
        share_ref[code : code + 1, :] = share_all[code, 0:1, :]
    for g, out in ((1, down_ref), (0, up_ref)):
        core_copy[g, 0].wait_recv()
        mine = part[g, 0].astype(f32) + from_core[g, 0].astype(f32)
        x_copy[g].wait_recv()
        out[...] = (mine + from_x[g].astype(f32)).astype(bf16)
    for copy in sent:
        copy.wait_send()


def fused(cap, tokens, cotangent, routes, gates, w_gate, w_up, w_down):
    near = lax.axis_index("expert") // SPLIT
    flat, slot = slot_of(routes, 2)
    ids = jnp.arange(2 * cap, dtype=jnp.int32)
    named = jnp.where(ids < cap, near, 1 - near)
    placed = (flat[None, :] == named[:, None]) & (slot[None, :] == (ids % cap)[:, None])
    hot = placed.astype(jnp.bfloat16)
    weight = gates.reshape(-1)
    hot_gate = jnp.where(placed, weight[None, :], jnp.zeros((), jnp.bfloat16))
    width = tokens.shape[1]
    hidden, cols = w_gate.shape
    count = 8 * cap
    bf16, f32 = jnp.bfloat16, jnp.float32
    vmem = pl.BlockSpec(memory_space=pltpu.VMEM)
    anywhere = pl.BlockSpec(memory_space=pl.ANY)
    dma = pltpu.SemaphoreType.DMA
    up, down, share = pl.pallas_call(
        lambda *refs: fused_kernel(cap, *refs),
        out_shape=(
            jax.ShapeDtypeStruct((hidden, cols), bf16),
            jax.ShapeDtypeStruct((hidden, cols), bf16),
            jax.ShapeDtypeStruct((8, count), f32),
        ),
        in_specs=[vmem] * 4 + [anywhere] * 3,
        out_specs=(vmem, vmem, vmem),
        scratch_shapes=[
            pltpu.VMEM((count, width), bf16),
            pltpu.VMEM((count, width), bf16),
            pltpu.VMEM((cap, width), bf16),
            pltpu.VMEM((cap, width), bf16),
            pltpu.VMEM((3, hidden, width), bf16),
            pltpu.VMEM((hidden, count), f32),
            pltpu.VMEM((hidden, count), f32),
            pltpu.VMEM((hidden, count), f32),
            pltpu.VMEM((hidden, count), bf16),
            pltpu.VMEM((hidden, count), bf16),
            pltpu.VMEM((2, 4, hidden, cols), bf16),
            pltpu.VMEM((2, 2, hidden, cols), bf16),
            pltpu.VMEM((2, hidden, cols), bf16),
            pltpu.VMEM((2, hidden, cols), bf16),
            pltpu.VMEM((8, count), f32),
            pltpu.VMEM((8, 8, count), f32),
            dma((3,)),
            dma((2, 8)), dma((2, 8)),
            dma((3, 3)), dma((3, 3)),
            dma((2, 2)), dma((2, 2)),
            dma((2,)), dma((2,)),
            dma((8,)), dma((8,)),
        ],
        compiler_params=pltpu.CompilerParams(
            collective_id=0, has_side_effects=True, vmem_limit_bytes=58 * 1024 * 1024
        ),
    )(hot, hot_gate, tokens, cotangent, w_gate, w_up, w_down)
    sums = []
    for codes in (range(4), range(4, 8)):
        sums.append(sum(share[c, PLACE[c] * cap : (PLACE[c] + 1) * cap] for c in codes))
    summed = jnp.concatenate(sums)
    gate_grad = jnp.sum(jnp.where(placed, summed[:, None], 0.0), axis=0)
    gate_grad = gate_grad / weight.astype(f32)
    return up, down, gate_grad.reshape(tokens.shape[0], TOP)


def partner(array, axis, bit):
    return lax.ppermute(array, axis, [(i, i ^ 1 << bit) for i in range(lax.axis_size(axis))])


def slot_of(routes, experts):
    flat = routes.reshape(-1)
    owner = (flat[:, None] == jnp.arange(experts, dtype=jnp.int32)[None, :]).astype(jnp.int32)
    before = jnp.cumsum(owner, axis=0) - owner
    slot = jnp.sum(before * owner, axis=1)
    return (flat, slot)


def shards(tokens, cotangent, routes, gates, w_gate, w_up, w_down):
    tok_count = tokens.shape[0]
    groups = lax.axis_size("expert")
    experts = groups // SPLIT
    capacity = max(2, min(TOK_DEV, 5 * TOK_DEV * TOP // (4 * experts)))
    if groups == 8 and lax.axis_size("dp") == 4 and capacity % 16 == 0 and capacity > 64:
        return fused(capacity, tokens, cotangent, routes, gates, w_gate, w_up, w_down)
    piece = (capacity + SPLIT - 1) // SPLIT
    levels = SPLIT.bit_length() - 1
    here = lax.axis_index("expert")
    flat, slot = slot_of(routes, experts)
    pair_count = flat.shape[0]
    pair_tok = (
        (jnp.arange(pair_count, dtype=jnp.int32) // TOP)[:, None]
        == jnp.arange(tok_count, dtype=jnp.int32)[None, :]
    ).astype(jnp.bfloat16)
    rows_all = groups * piece
    row_ids = jnp.arange(rows_all, dtype=jnp.int32)
    dest = row_ids // piece
    row_expert = dest // SPLIT
    row_slot = dest % SPLIT + row_ids % piece * SPLIT
    placed = (flat[None, :] == row_expert[:, None]) & (slot[None, :] == row_slot[:, None])
    placed_f = placed.astype(jnp.float32)
    token_map = jnp.dot(
        placed.astype(jnp.bfloat16), pair_tok, preferred_element_type=jnp.float32
    ).astype(jnp.bfloat16)
    send_x = jnp.dot(token_map, tokens, preferred_element_type=jnp.float32).astype(jnp.bfloat16)
    send_dy = jnp.dot(token_map, cotangent, preferred_element_type=jnp.float32).astype(jnp.bfloat16)
    send_gate = jnp.dot(
        placed_f, gates.reshape(-1).astype(jnp.float32), precision=lax.Precision.HIGHEST
    ).astype(jnp.bfloat16)
    full_gate, full_up, full_down = (
        lax.all_gather(w_gate, "dp", axis=1, tiled=True),
        lax.all_gather(w_up, "dp", axis=1, tiled=True),
        lax.all_gather(w_down, "dp", axis=1, tiled=True),
    )
    cur_x, cur_dy, cur_g = (
        lax.all_to_all(send_x, "expert", split_axis=0, concat_axis=0, tiled=True),
        lax.all_to_all(send_dy, "expert", split_axis=0, concat_axis=0, tiled=True),
        lax.all_to_all(send_gate, "expert", split_axis=0, concat_axis=0, tiled=True),
    )
    for bit in range(levels):
        got = partner((cur_x, cur_dy, cur_g), "expert", bit)
        lower = here // (1 << bit) % 2 == 0
        cur_x = jnp.where(
            lower,
            jnp.concatenate([cur_x, got[0]], axis=0),
            jnp.concatenate([got[0], cur_x], axis=0),
        )
        cur_dy = jnp.where(
            lower,
            jnp.concatenate([cur_dy, got[1]], axis=0),
            jnp.concatenate([got[1], cur_dy], axis=0),
        )
        cur_g = jnp.where(
            lower,
            jnp.concatenate([cur_g, got[2]], axis=0),
            jnp.concatenate([got[2], cur_g], axis=0),
        )
    rows_x, rows_dy, recv_gate = (cur_x, cur_dy, cur_g)
    pre_a = lax.dot_general(
        rows_x, full_gate, (((1,), (1,)), ((), ())), preferred_element_type=jnp.float32
    )
    pre_b = lax.dot_general(
        rows_x, full_up, (((1,), (1,)), ((), ())), preferred_element_type=jnp.float32
    )
    sig = jax.nn.sigmoid(pre_a)
    silu = pre_a * sig
    hidden = (silu * pre_b).astype(jnp.bfloat16)
    weight = recv_gate.astype(jnp.float32)
    probe = lax.dot_general(
        rows_dy, full_down, (((1,), (1,)), ((), ())), preferred_element_type=jnp.float32
    )
    share = jnp.sum(hidden.astype(jnp.float32) * probe, axis=1)
    scaled = (weight[:, None] * rows_dy.astype(jnp.float32)).astype(jnp.bfloat16)
    d_b = (weight[:, None] * probe * silu).astype(jnp.bfloat16)
    part_up = lax.dot_general(
        d_b, rows_x, (((0,), (0,)), ((), ())), preferred_element_type=jnp.float32
    )
    part_down = lax.dot_general(
        hidden, scaled, (((0,), (0,)), ((), ())), preferred_element_type=jnp.float32
    )
    folded = share.reshape(SPLIT, rows_all)
    for bit in reversed(range(levels)):
        half = folded.shape[0] // 2
        lower_half = folded[:half]
        upper_half = folded[half:]
        lower = here // (1 << bit) % 2 == 0
        keep = jnp.where(lower, lower_half, upper_half)
        away = jnp.where(lower, upper_half, lower_half)
        folded = keep + partner(away, "expert", bit)
    summed = lax.all_to_all(
        folded.reshape(rows_all), "expert", split_axis=0, concat_axis=0, tiled=True
    )
    gate_grad = jnp.dot(placed_f.T, summed, precision=lax.Precision.HIGHEST)
    sum_up, sum_down = (
        lax.psum_scatter(
            part_up.astype(jnp.bfloat16), "dp", scatter_dimension=1, tiled=True
        ).astype(jnp.float32),
        lax.psum_scatter(
            part_down.astype(jnp.bfloat16), "dp", scatter_dimension=1, tiled=True
        ).astype(jnp.float32),
    )
    return (
        sum_up.astype(jnp.bfloat16),
        sum_down.astype(jnp.bfloat16),
        gate_grad.reshape(tok_count, TOP),
    )


def solution(mesh):
    in_specs = (
        P(("expert", "dp"), None),
        P(("expert", "dp"), None),
        P(("expert", "dp"), None),
        P(("expert", "dp"), None),
        P("expert", "dp"),
        P("expert", "dp"),
        P("expert", "dp"),
    )
    out_specs = (P("expert", "dp"), P("expert", "dp"), P(("expert", "dp"), None))
    return jax.shard_map(shards, mesh=mesh, in_specs=in_specs, out_specs=out_specs, check_vma=False)
```

```python
import jax
import jax.numpy as jnp
from jax import lax
from jax.experimental import pallas as pl
from jax.experimental.pallas import tpu as pltpu
from jax.sharding import PartitionSpec as P

SPLIT = 4
TOP = 1
TOK_DEV = 128
MESH = pl.DeviceIdType.MESH
ORDER = (0, 4, 1, 5)
PLACE = {c: i for i, c in enumerate(ORDER)}


def flip(index, code):
    for bit in (1, 2, 4):
        if code & bit:
            index = index + bit - 2 * bit * ((index // bit) % 2)
    return index


def fused_kernel(
    cap, oh_ref, ohg_ref, tok_ref, cot_ref, wg_ref, wu_ref, wd_ref,
    up_ref, down_ref, share_ref,
    rows_x, rows_c, far_x, far_c, w_all, t_a, t_b, t_p, t_h, t_d,
    part, from_core, to_first, from_first, to_second, from_second, share_mine, share_all,
    local_sem, row_send, row_recv, w_send, w_recv, core_send, core_recv,
    first_send, first_recv, second_send, second_recv, share_send, share_recv,
):
    e = lax.axis_index("expert")
    d = lax.axis_index("dp")
    hidden, cols = wg_ref.shape
    nt = (((1,), (1,)), ((), ()))
    nn = (((1,), (0,)), ((), ()))
    f32, bf16 = jnp.float32, jnp.bfloat16
    to_y, to_z = {"expert": flip(e, 1)}, {"expert": flip(e, 2)}
    to_core_dev, to_x = {"dp": flip(d, 1)}, {"dp": flip(d, 2)}

    barrier = pltpu.get_barrier_semaphore()
    for code in (1, 2, 4, 5):
        pl.semaphore_signal(barrier, inc=1, device_id={"expert": flip(e, code)}, device_id_type=MESH)
    for code in (1, 2):
        pl.semaphore_signal(barrier, inc=1, device_id={"dp": flip(d, code)}, device_id_type=MESH)
    pl.semaphore_wait(barrier, 6)

    sent = []

    def push(src, dst, send_sem, recv_sem, device):
        copy = pltpu.make_async_remote_copy(
            src_ref=src, dst_ref=dst, send_sem=send_sem, recv_sem=recv_sem,
            device_id=device, device_id_type=MESH,
        )
        copy.start()
        sent.append(copy)
        return copy

    def band(index):
        return pl.ds(pl.multiple_of(index * cols, 128), cols)

    w_in = (wg_ref, wu_ref, wd_ref)
    w_copy = {}

    def w_at(k, part_of, code):
        return w_all.at[k, part_of * hidden : (part_of + 1) * hidden, band(flip(d, code))]

    def w_push(k, source, code, device, there, there_code):
        number = there * 4 + there_code
        w_copy[k, there, there_code] = push(
            source, w_all.at[k, there * hidden : (there + 1) * hidden, band(flip(d, code))],
            w_send.at[k, number], w_recv.at[k, number], device,
        )

    local = []

    def w_own(k):
        w_push(k, w_in[k], 0, to_z, 1, 0)
        w_push(k, w_in[k], 0, to_x, 0, 2)
        w_push(k, w_in[k], 0, to_core_dev, 0, 1)
        here = pltpu.make_async_copy(w_in[k], w_at(k, 0, 0), local_sem.at[k])
        here.start()
        local.append(here)

    def w_first(k):
        w_copy[k, 1, 0].wait_recv()
        w_push(k, w_at(k, 1, 0), 0, to_x, 1, 2)
        w_push(k, w_at(k, 1, 0), 0, to_core_dev, 1, 1)
        w_copy[k, 0, 2].wait_recv()
        w_push(k, w_at(k, 0, 2), 2, to_core_dev, 0, 3)

    def w_last(k):
        w_copy[k, 1, 2].wait_recv()
        w_push(k, w_at(k, 1, 2), 2, to_core_dev, 1, 3)

    def w_ready(k):
        local[k].wait()
        for key in ((0, 1), (1, 1), (0, 3), (1, 3)):
            w_copy[(k,) + key].wait_recv()

    def at(ref, code):
        return ref.at[pl.ds(PLACE[code] * cap, cap), :]

    rows = (rows_x, rows_c)
    row_copy = {}

    def send_row(kind, slot, hop, source=None):
        there = slot ^ hop
        row_copy[kind, there] = push(
            at(rows[kind], slot) if source is None else source, at(rows[kind], there),
            row_send.at[kind, there], row_recv.at[kind, there], {"expert": flip(e, hop)},
        )

    def got(kind, code):
        row_copy[kind, code].wait_recv()

    def pick(hot, source):
        return lax.dot_general(hot, source, nn, preferred_element_type=f32).astype(bf16)

    w_own(0)
    for kind, hot, source, far in ((0, oh_ref, tok_ref, far_x), (1, ohg_ref, cot_ref, far_c)):
        far[...] = pick(hot[cap:, :], source[...])
        send_row(kind, 0, 4, far)
        at(rows[kind], 0)[...] = pick(hot[:cap, :], source[...])
        send_row(kind, 0, 1)
        w_own(kind + 1)

    def project(dst, k, kind):
        for i in range(2):
            dst[i * hidden : (i + 1) * hidden, :] = lax.dot_general(
                w_all[k, i * hidden : (i + 1) * hidden, :], rows[kind][...], nt, preferred_element_type=f32
            )

    left = (t_d, t_h)
    right = (rows_x, rows_c)

    def block(g, i, code):
        part[g, i, code] = lax.dot_general(
            left[g][i * hidden : (i + 1) * hidden, :], right[g][:, band(flip(d, code))], nn,
            preferred_element_type=f32,
        ).astype(bf16)

    core_copy = {}
    first_copy = {}
    second_copy = {}

    def to_core(g, i, code):
        block(g, i, code)
        n = code // 2
        core_copy[g, i, n] = push(
            part.at[g, i, code], from_core.at[g, i, n],
            core_send.at[g, i * 2 + n], core_recv.at[g, i * 2 + n], to_core_dev,
        )

    def both(g, i, n):
        core_copy[g, i, n].wait_recv()
        return part[g, i, 2 * n].astype(f32) + from_core[g, i, n].astype(f32)

    def first(g, i, n, number, device):
        to_first[g, number] = both(g, i, n).astype(bf16)
        first_copy[g, number] = push(
            to_first.at[g, number], from_first.at[g, number],
            first_send.at[g, number], first_recv.at[g, number], device,
        )

    def second(g, i, n, device):
        mine = both(g, i, n)
        first_copy[g, 1].wait_recv()
        to_second[g] = (mine + from_first[g, 1].astype(f32)).astype(bf16)
        second_copy[g] = push(
            to_second.at[g], from_second.at[g], second_send.at[g], second_recv.at[g], device
        )

    got(0, 4)
    send_row(0, 4, 1)
    w_first(0)
    w_first(1)
    got(1, 4)
    send_row(1, 4, 1)
    w_first(2)
    w_last(0)
    w_last(1)
    got(0, 1)
    got(0, 5)
    w_ready(0)
    project(t_a, 0, 0)
    w_ready(1)
    project(t_b, 1, 0)
    a = t_a[...]
    silu = a * jax.nn.sigmoid(a)
    t_h[...] = (silu * t_b[...]).astype(bf16)
    t_a[...] = silu
    got(1, 1)
    got(1, 5)

    to_core(1, 1, 3)
    to_core(1, 1, 1)
    block(1, 1, 2)
    block(1, 1, 0)
    first(1, 1, 1, 1, to_z)
    first(1, 1, 0, 0, to_z)
    w_last(2)
    to_core(1, 0, 3)
    to_core(1, 0, 1)
    block(1, 0, 2)
    block(1, 0, 0)
    w_ready(2)
    project(t_p, 2, 1)
    p = t_p[...]
    t_d[...] = (p * t_a[...]).astype(bf16)

    to_core(0, 1, 3)
    to_core(0, 0, 3)
    block(0, 1, 2)
    block(0, 0, 2)
    first(0, 1, 1, 1, to_x)
    first(0, 0, 1, 0, to_x)
    second(1, 0, 1, to_x)
    to_core(0, 1, 1)
    to_core(0, 0, 1)
    block(0, 1, 0)
    block(0, 0, 0)

    total = jnp.sum(t_h[...].astype(f32) * t_p[...], axis=0, keepdims=True)
    share_mine[...] = jnp.broadcast_to(total, share_mine.shape)
    share_copy = {}
    for code in (1, 4, 5):
        n = PLACE[code]
        share_copy[n] = push(
            share_mine, share_all.at[n], share_send.at[n], share_recv.at[n], {"expert": flip(e, code)}
        )
    second(0, 1, 0, to_z)
    share_ref[0:1, :] = share_mine[0:1, :]
    for n in (1, 2, 3):
        share_copy[n].wait_recv()
        share_ref[n : n + 1, :] = share_all[n, 0:1, :]
    for g, out in ((1, down_ref), (0, up_ref)):
        core_copy[g, 0, 0].wait_recv()
        mine = part[g, 0, 0].astype(f32) + from_core[g, 0, 0].astype(f32)
        first_copy[g, 0].wait_recv()
        mine = mine + from_first[g, 0].astype(f32)
        second_copy[g].wait_recv()
        out[...] = (mine + from_second[g].astype(f32)).astype(bf16)
    for copy in sent:
        copy.wait_send()


def fused(cap, tokens, cotangent, routes, gates, w_gate, w_up, w_down):
    near = lax.axis_index("expert") // SPLIT
    flat, slot = slot_of(routes, 2)
    ids = jnp.arange(2 * cap, dtype=jnp.int32)
    named = jnp.where(ids < cap, near, 1 - near)
    placed = (flat[None, :] == named[:, None]) & (slot[None, :] == (ids % cap)[:, None])
    hot = placed.astype(jnp.bfloat16)
    weight = gates.reshape(-1)
    hot_gate = jnp.where(placed, weight[None, :], jnp.zeros((), jnp.bfloat16))
    width = tokens.shape[1]
    hidden, cols = w_gate.shape
    count = len(ORDER) * cap
    bf16, f32 = jnp.bfloat16, jnp.float32
    vmem = pl.BlockSpec(memory_space=pltpu.VMEM)
    anywhere = pl.BlockSpec(memory_space=pl.ANY)
    dma = pltpu.SemaphoreType.DMA
    up, down, share = pl.pallas_call(
        lambda *refs: fused_kernel(cap, *refs),
        out_shape=(
            jax.ShapeDtypeStruct((hidden, cols), bf16),
            jax.ShapeDtypeStruct((hidden, cols), bf16),
            jax.ShapeDtypeStruct((4, count), f32),
        ),
        in_specs=[vmem] * 4 + [anywhere] * 3,
        out_specs=(vmem, vmem, vmem),
        scratch_shapes=[
            pltpu.VMEM((count, width), bf16),
            pltpu.VMEM((count, width), bf16),
            pltpu.VMEM((cap, width), bf16),
            pltpu.VMEM((cap, width), bf16),
            pltpu.VMEM((3, 2 * hidden, width), bf16),
            pltpu.VMEM((2 * hidden, count), f32),
            pltpu.VMEM((2 * hidden, count), f32),
            pltpu.VMEM((2 * hidden, count), f32),
            pltpu.VMEM((2 * hidden, count), bf16),
            pltpu.VMEM((2 * hidden, count), bf16),
            pltpu.VMEM((2, 2, 4, hidden, cols), bf16),
            pltpu.VMEM((2, 2, 2, hidden, cols), bf16),
            pltpu.VMEM((2, 2, hidden, cols), bf16),
            pltpu.VMEM((2, 2, hidden, cols), bf16),
            pltpu.VMEM((2, hidden, cols), bf16),
            pltpu.VMEM((2, hidden, cols), bf16),
            pltpu.VMEM((8, count), f32),
            pltpu.VMEM((4, 8, count), f32),
            dma((3,)),
            dma((2, 8)), dma((2, 8)),
            dma((3, 8)), dma((3, 8)),
            dma((2, 4)), dma((2, 4)),
            dma((2, 2)), dma((2, 2)),
            dma((2,)), dma((2,)),
            dma((4,)), dma((4,)),
        ],
        compiler_params=pltpu.CompilerParams(
            collective_id=0, has_side_effects=True, vmem_limit_bytes=60 * 1024 * 1024
        ),
    )(hot, hot_gate, tokens, cotangent, w_gate, w_up, w_down)
    sums = []
    for codes in ((0, 1), (4, 5)):
        sums.append(sum(share[PLACE[c], PLACE[c] * cap : (PLACE[c] + 1) * cap] for c in codes))
    summed = jnp.concatenate(sums)
    gate_grad = jnp.sum(jnp.where(placed, summed[:, None], 0.0), axis=0)
    gate_grad = gate_grad / weight.astype(f32)
    return up, down, gate_grad.reshape(tokens.shape[0], TOP)


def partner(array, axis, bit):
    return lax.ppermute(array, axis, [(i, i ^ 1 << bit) for i in range(lax.axis_size(axis))])


def slot_of(routes, experts):
    flat = routes.reshape(-1)
    owner = (flat[:, None] == jnp.arange(experts, dtype=jnp.int32)[None, :]).astype(jnp.int32)
    before = jnp.cumsum(owner, axis=0) - owner
    slot = jnp.sum(before * owner, axis=1)
    return (flat, slot)


def shards(tokens, cotangent, routes, gates, w_gate, w_up, w_down):
    tok_count = tokens.shape[0]
    groups = lax.axis_size("expert")
    experts = groups // SPLIT
    capacity = max(2, min(TOK_DEV, 5 * TOK_DEV * TOP // (4 * experts)))
    if groups == 8 and lax.axis_size("dp") == 4 and capacity % 16 == 0 and capacity > 64:
        return fused(capacity, tokens, cotangent, routes, gates, w_gate, w_up, w_down)
    piece = (capacity + SPLIT - 1) // SPLIT
    levels = SPLIT.bit_length() - 1
    here = lax.axis_index("expert")
    flat, slot = slot_of(routes, experts)
    pair_count = flat.shape[0]
    pair_tok = (
        (jnp.arange(pair_count, dtype=jnp.int32) // TOP)[:, None]
        == jnp.arange(tok_count, dtype=jnp.int32)[None, :]
    ).astype(jnp.bfloat16)
    rows_all = groups * piece
    row_ids = jnp.arange(rows_all, dtype=jnp.int32)
    dest = row_ids // piece
    row_expert = dest // SPLIT
    row_slot = dest % SPLIT + row_ids % piece * SPLIT
    placed = (flat[None, :] == row_expert[:, None]) & (slot[None, :] == row_slot[:, None])
    placed_f = placed.astype(jnp.float32)
    token_map = jnp.dot(
        placed.astype(jnp.bfloat16), pair_tok, preferred_element_type=jnp.float32
    ).astype(jnp.bfloat16)
    send_x = jnp.dot(token_map, tokens, preferred_element_type=jnp.float32).astype(jnp.bfloat16)
    send_dy = jnp.dot(token_map, cotangent, preferred_element_type=jnp.float32).astype(jnp.bfloat16)
    send_gate = jnp.dot(
        placed_f, gates.reshape(-1).astype(jnp.float32), precision=lax.Precision.HIGHEST
    ).astype(jnp.bfloat16)
    full_gate, full_up, full_down = (
        lax.all_gather(w_gate, "dp", axis=1, tiled=True),
        lax.all_gather(w_up, "dp", axis=1, tiled=True),
        lax.all_gather(w_down, "dp", axis=1, tiled=True),
    )
    cur_x, cur_dy, cur_g = (
        lax.all_to_all(send_x, "expert", split_axis=0, concat_axis=0, tiled=True),
        lax.all_to_all(send_dy, "expert", split_axis=0, concat_axis=0, tiled=True),
        lax.all_to_all(send_gate, "expert", split_axis=0, concat_axis=0, tiled=True),
    )
    for bit in range(levels):
        got = partner((cur_x, cur_dy, cur_g), "expert", bit)
        lower = here // (1 << bit) % 2 == 0
        cur_x = jnp.where(
            lower,
            jnp.concatenate([cur_x, got[0]], axis=0),
            jnp.concatenate([got[0], cur_x], axis=0),
        )
        cur_dy = jnp.where(
            lower,
            jnp.concatenate([cur_dy, got[1]], axis=0),
            jnp.concatenate([got[1], cur_dy], axis=0),
        )
        cur_g = jnp.where(
            lower,
            jnp.concatenate([cur_g, got[2]], axis=0),
            jnp.concatenate([got[2], cur_g], axis=0),
        )
    rows_x, rows_dy, recv_gate = (cur_x, cur_dy, cur_g)
    pre_a = lax.dot_general(
        rows_x, full_gate, (((1,), (1,)), ((), ())), preferred_element_type=jnp.float32
    )
    pre_b = lax.dot_general(
        rows_x, full_up, (((1,), (1,)), ((), ())), preferred_element_type=jnp.float32
    )
    sig = jax.nn.sigmoid(pre_a)
    silu = pre_a * sig
    hidden = (silu * pre_b).astype(jnp.bfloat16)
    weight = recv_gate.astype(jnp.float32)
    probe = lax.dot_general(
        rows_dy, full_down, (((1,), (1,)), ((), ())), preferred_element_type=jnp.float32
    )
    share = jnp.sum(hidden.astype(jnp.float32) * probe, axis=1)
    scaled = (weight[:, None] * rows_dy.astype(jnp.float32)).astype(jnp.bfloat16)
    d_b = (weight[:, None] * probe * silu).astype(jnp.bfloat16)
    part_up = lax.dot_general(
        d_b, rows_x, (((0,), (0,)), ((), ())), preferred_element_type=jnp.float32
    )
    part_down = lax.dot_general(
        hidden, scaled, (((0,), (0,)), ((), ())), preferred_element_type=jnp.float32
    )
    folded = share.reshape(SPLIT, rows_all)
    for bit in reversed(range(levels)):
        half = folded.shape[0] // 2
        lower_half = folded[:half]
        upper_half = folded[half:]
        lower = here // (1 << bit) % 2 == 0
        keep = jnp.where(lower, lower_half, upper_half)
        away = jnp.where(lower, upper_half, lower_half)
        folded = keep + partner(away, "expert", bit)
    summed = lax.all_to_all(
        folded.reshape(rows_all), "expert", split_axis=0, concat_axis=0, tiled=True
    )
    gate_grad = jnp.dot(placed_f.T, summed, precision=lax.Precision.HIGHEST)
    sum_up, sum_down = (
        lax.psum_scatter(
            part_up.astype(jnp.bfloat16), "dp", scatter_dimension=1, tiled=True
        ).astype(jnp.float32),
        lax.psum_scatter(
            part_down.astype(jnp.bfloat16), "dp", scatter_dimension=1, tiled=True
        ).astype(jnp.float32),
    )
    return (
        sum_up.astype(jnp.bfloat16),
        sum_down.astype(jnp.bfloat16),
        gate_grad.reshape(tok_count, TOP),
    )


def solution(mesh):
    in_specs = (
        P(("expert", "dp"), None),
        P(("expert", "dp"), None),
        P(("expert", "dp"), None),
        P(("expert", "dp"), None),
        P("expert", "dp"),
        P("expert", "dp"),
        P("expert", "dp"),
    )
    out_specs = (P("expert", "dp"), P("expert", "dp"), P(("expert", "dp"), None))
    return jax.shard_map(shards, mesh=mesh, in_specs=in_specs, out_specs=out_specs, check_vma=False)
```

```python
import jax
import jax.numpy as jnp
from jax import lax
from jax.experimental import pallas as pl
from jax.experimental.pallas import tpu as pltpu
from jax.sharding import PartitionSpec as P

SPLIT = 4
TOP = 1
TOK_DEV = 128
MESH = pl.DeviceIdType.MESH
PIECES = 4
ORDER = (0, 4, 1, 5)
PLACE = {c: i for i, c in enumerate(ORDER)}


def flip(index, code):
    for bit in (1, 2, 4):
        if code & bit:
            index = index + bit - 2 * bit * ((index // bit) % 2)
    return index


def fused_kernel(
    cap, oh_ref, ohg_ref, tok_ref, cot_ref, wg_ref, wu_ref, wd_ref,
    up_ref, down_ref, share_ref,
    rows_x, rows_c, far_x, far_c, w_all, t_a, t_b, t_p, t_h, t_d,
    part, from_core, to_first, from_first, to_second, from_second, share_mine, share_all,
    local_sem, row_send, row_recv, w_send, w_recv, core_send, core_recv,
    first_send, first_recv, second_send, second_recv, share_send, share_recv,
):
    e = lax.axis_index("expert")
    d = lax.axis_index("dp")
    hidden, cols = wg_ref.shape
    nt = (((1,), (1,)), ((), ()))
    nn = (((1,), (0,)), ((), ()))
    f32, bf16 = jnp.float32, jnp.bfloat16
    to_y, to_z = {"expert": flip(e, 1)}, {"expert": flip(e, 2)}
    to_core_dev, to_x = {"dp": flip(d, 1)}, {"dp": flip(d, 2)}

    barrier = pltpu.get_barrier_semaphore()
    for code in (1, 2, 4, 5):
        pl.semaphore_signal(barrier, inc=1, device_id={"expert": flip(e, code)}, device_id_type=MESH)
    for code in (1, 2):
        pl.semaphore_signal(barrier, inc=1, device_id={"dp": flip(d, code)}, device_id_type=MESH)
    pl.semaphore_wait(barrier, 6)

    sent = []

    def push(src, dst, send_sem, recv_sem, device):
        copy = pltpu.make_async_remote_copy(
            src_ref=src, dst_ref=dst, send_sem=send_sem, recv_sem=recv_sem,
            device_id=device, device_id_type=MESH,
        )
        copy.start()
        sent.append(copy)
        return copy

    def band(index):
        return pl.ds(pl.multiple_of(index * cols, 128), cols)

    w_in = (wg_ref, wu_ref, wd_ref)
    w_copy = {}

    def w_at(k, part_of, code):
        return w_all.at[k, part_of * hidden : (part_of + 1) * hidden, band(flip(d, code))]

    def w_push(k, source, code, device, there, there_code):
        number = there * 4 + there_code
        w_copy[k, there, there_code] = push(
            source, w_all.at[k, there * hidden : (there + 1) * hidden, band(flip(d, code))],
            w_send.at[k, number], w_recv.at[k, number], device,
        )

    local = []

    def w_own(k):
        w_push(k, w_in[k], 0, to_z, 1, 0)
        w_push(k, w_in[k], 0, to_x, 0, 2)
        w_push(k, w_in[k], 0, to_core_dev, 0, 1)
        here = pltpu.make_async_copy(w_in[k], w_at(k, 0, 0), local_sem.at[k])
        here.start()
        local.append(here)

    def w_first(k):
        w_copy[k, 1, 0].wait_recv()
        w_push(k, w_at(k, 1, 0), 0, to_x, 1, 2)
        w_push(k, w_at(k, 1, 0), 0, to_core_dev, 1, 1)
        w_copy[k, 0, 2].wait_recv()
        w_push(k, w_at(k, 0, 2), 2, to_core_dev, 0, 3)

    def w_last(k):
        w_copy[k, 1, 2].wait_recv()
        w_push(k, w_at(k, 1, 2), 2, to_core_dev, 1, 3)

    def w_ready(k):
        local[k].wait()
        for key in ((0, 1), (1, 1), (0, 3), (1, 3)):
            w_copy[(k,) + key].wait_recv()

    step = rows_x.shape[1] // PIECES

    def at(ref, code, piece):
        return ref.at[pl.ds(PLACE[code] * cap, cap), pl.ds(piece * step, step)]

    rows = (rows_x, rows_c)
    row_copy = {}

    def send_row(kind, slot, hop, piece, source=None):
        there = slot ^ hop
        row_copy[kind, there, piece] = push(
            at(rows[kind], slot, piece) if source is None else source, at(rows[kind], there, piece),
            row_send.at[kind, there, piece], row_recv.at[kind, there, piece], {"expert": flip(e, hop)},
        )

    def got(kind, code, piece):
        row_copy[kind, code, piece].wait_recv()

    def got_all(kind, code):
        for piece in range(PIECES):
            got(kind, code, piece)

    hots = (oh_ref, ohg_ref)
    whole = (tok_ref, cot_ref)
    fars = (far_x, far_c)

    def pick(kind, low, piece):
        return lax.dot_general(
            hots[kind][low : low + cap, :], whole[kind][:, piece * step : (piece + 1) * step], nn,
            preferred_element_type=f32,
        ).astype(bf16)

    def send_far(kind, piece):
        lanes = pl.ds(piece * step, step)
        fars[kind][:, lanes] = pick(kind, cap, piece)
        send_row(kind, 0, 4, piece, fars[kind].at[:, lanes])

    def send_near(kind, piece):
        at(rows[kind], 0, piece)[...] = pick(kind, 0, piece)
        send_row(kind, 0, 1, piece)

    def pass_on(kind, piece):
        got(kind, 4, piece)
        send_row(kind, 4, 1, piece)

    send_far(0, 0)
    send_near(0, 0)
    send_far(0, 1)
    w_own(0)
    send_near(0, 1)
    send_far(0, 2)
    send_near(0, 2)
    send_far(0, 3)
    send_near(0, 3)
    w_own(1)
    send_far(1, 0)
    send_near(1, 0)
    send_far(1, 1)
    send_near(1, 1)
    w_own(2)
    send_far(1, 2)
    send_near(1, 2)
    send_far(1, 3)
    send_near(1, 3)

    def project(dst, k, kind):
        for i in range(2):
            dst[i * hidden : (i + 1) * hidden, :] = lax.dot_general(
                w_all[k, i * hidden : (i + 1) * hidden, :], rows[kind][...], nt, preferred_element_type=f32
            )

    left = (t_d, t_h)
    right = (rows_x, rows_c)

    def block(g, i, code):
        part[g, i, code] = lax.dot_general(
            left[g][i * hidden : (i + 1) * hidden, :], right[g][:, band(flip(d, code))], nn,
            preferred_element_type=f32,
        ).astype(bf16)

    core_copy = {}
    first_copy = {}
    second_copy = {}

    def to_core(g, i, code):
        block(g, i, code)
        n = code // 2
        core_copy[g, i, n] = push(
            part.at[g, i, code], from_core.at[g, i, n],
            core_send.at[g, i * 2 + n], core_recv.at[g, i * 2 + n], to_core_dev,
        )

    def both(g, i, n):
        core_copy[g, i, n].wait_recv()
        return part[g, i, 2 * n].astype(f32) + from_core[g, i, n].astype(f32)

    def first(g, i, n, number, device):
        to_first[g, number] = both(g, i, n).astype(bf16)
        first_copy[g, number] = push(
            to_first.at[g, number], from_first.at[g, number],
            first_send.at[g, number], first_recv.at[g, number], device,
        )

    def second(g, i, n, device):
        mine = both(g, i, n)
        first_copy[g, 1].wait_recv()
        to_second[g] = (mine + from_first[g, 1].astype(f32)).astype(bf16)
        second_copy[g] = push(
            to_second.at[g], from_second.at[g], second_send.at[g], second_recv.at[g], device
        )

    pass_on(0, 0)
    pass_on(0, 1)
    w_first(0)
    pass_on(0, 2)
    pass_on(0, 3)
    w_first(1)
    pass_on(1, 0)
    pass_on(1, 1)
    w_last(0)
    w_first(2)
    pass_on(1, 2)
    pass_on(1, 3)
    w_last(1)
    got_all(0, 1)
    got_all(0, 5)
    w_ready(0)
    project(t_a, 0, 0)
    w_ready(1)
    project(t_b, 1, 0)
    a = t_a[...]
    silu = a * jax.nn.sigmoid(a)
    t_h[...] = (silu * t_b[...]).astype(bf16)
    t_a[...] = silu
    got_all(1, 1)
    got_all(1, 5)

    to_core(1, 1, 3)
    to_core(1, 1, 1)
    block(1, 1, 2)
    block(1, 1, 0)
    first(1, 1, 1, 1, to_z)
    first(1, 1, 0, 0, to_z)
    w_last(2)
    to_core(1, 0, 3)
    to_core(1, 0, 1)
    block(1, 0, 2)
    block(1, 0, 0)
    w_ready(2)
    project(t_p, 2, 1)
    p = t_p[...]
    t_d[...] = (p * t_a[...]).astype(bf16)

    to_core(0, 1, 3)
    to_core(0, 0, 3)
    block(0, 1, 2)
    block(0, 0, 2)
    first(0, 1, 1, 1, to_x)
    second(1, 0, 1, to_x)
    first(0, 0, 1, 0, to_x)
    to_core(0, 1, 1)
    to_core(0, 0, 1)
    block(0, 1, 0)
    block(0, 0, 0)

    total = jnp.sum(t_h[...].astype(f32) * t_p[...], axis=0, keepdims=True)
    share_mine[...] = jnp.broadcast_to(total, share_mine.shape)
    share_copy = {}
    for code in (1, 4, 5):
        n = PLACE[code]
        share_copy[n] = push(
            share_mine, share_all.at[n], share_send.at[n], share_recv.at[n], {"expert": flip(e, code)}
        )
    second(0, 1, 0, to_z)
    share_ref[0:1, :] = share_mine[0:1, :]
    for n in (1, 2, 3):
        share_copy[n].wait_recv()
        share_ref[n : n + 1, :] = share_all[n, 0:1, :]
    for g, out in ((1, down_ref), (0, up_ref)):
        core_copy[g, 0, 0].wait_recv()
        mine = part[g, 0, 0].astype(f32) + from_core[g, 0, 0].astype(f32)
        first_copy[g, 0].wait_recv()
        mine = mine + from_first[g, 0].astype(f32)
        second_copy[g].wait_recv()
        out[...] = (mine + from_second[g].astype(f32)).astype(bf16)
    for copy in sent:
        copy.wait_send()


def fused(cap, tokens, cotangent, routes, gates, w_gate, w_up, w_down):
    near = lax.axis_index("expert") // SPLIT
    flat, slot = slot_of(routes, 2)
    ids = jnp.arange(2 * cap, dtype=jnp.int32)
    named = jnp.where(ids < cap, near, 1 - near)
    placed = (flat[None, :] == named[:, None]) & (slot[None, :] == (ids % cap)[:, None])
    hot = placed.astype(jnp.bfloat16)
    weight = gates.reshape(-1)
    hot_gate = jnp.where(placed, weight[None, :], jnp.zeros((), jnp.bfloat16))
    width = tokens.shape[1]
    hidden, cols = w_gate.shape
    count = len(ORDER) * cap
    bf16, f32 = jnp.bfloat16, jnp.float32
    vmem = pl.BlockSpec(memory_space=pltpu.VMEM)
    anywhere = pl.BlockSpec(memory_space=pl.ANY)
    dma = pltpu.SemaphoreType.DMA
    up, down, share = pl.pallas_call(
        lambda *refs: fused_kernel(cap, *refs),
        out_shape=(
            jax.ShapeDtypeStruct((hidden, cols), bf16),
            jax.ShapeDtypeStruct((hidden, cols), bf16),
            jax.ShapeDtypeStruct((4, count), f32),
        ),
        in_specs=[vmem] * 4 + [anywhere] * 3,
        out_specs=(vmem, vmem, vmem),
        scratch_shapes=[
            pltpu.VMEM((count, width), bf16),
            pltpu.VMEM((count, width), bf16),
            pltpu.VMEM((cap, width), bf16),
            pltpu.VMEM((cap, width), bf16),
            pltpu.VMEM((3, 2 * hidden, width), bf16),
            pltpu.VMEM((2 * hidden, count), f32),
            pltpu.VMEM((2 * hidden, count), f32),
            pltpu.VMEM((2 * hidden, count), f32),
            pltpu.VMEM((2 * hidden, count), bf16),
            pltpu.VMEM((2 * hidden, count), bf16),
            pltpu.VMEM((2, 2, 4, hidden, cols), bf16),
            pltpu.VMEM((2, 2, 2, hidden, cols), bf16),
            pltpu.VMEM((2, 2, hidden, cols), bf16),
            pltpu.VMEM((2, 2, hidden, cols), bf16),
            pltpu.VMEM((2, hidden, cols), bf16),
            pltpu.VMEM((2, hidden, cols), bf16),
            pltpu.VMEM((8, count), f32),
            pltpu.VMEM((4, 8, count), f32),
            dma((3,)),
            dma((2, 8, PIECES)), dma((2, 8, PIECES)),
            dma((3, 8)), dma((3, 8)),
            dma((2, 4)), dma((2, 4)),
            dma((2, 2)), dma((2, 2)),
            dma((2,)), dma((2,)),
            dma((4,)), dma((4,)),
        ],
        compiler_params=pltpu.CompilerParams(
            collective_id=0, has_side_effects=True, vmem_limit_bytes=60 * 1024 * 1024
        ),
    )(hot, hot_gate, tokens, cotangent, w_gate, w_up, w_down)
    sums = []
    for codes in ((0, 1), (4, 5)):
        sums.append(sum(share[PLACE[c], PLACE[c] * cap : (PLACE[c] + 1) * cap] for c in codes))
    summed = jnp.concatenate(sums)
    gate_grad = jnp.sum(jnp.where(placed, summed[:, None], 0.0), axis=0)
    gate_grad = gate_grad / weight.astype(f32)
    return up, down, gate_grad.reshape(tokens.shape[0], TOP)


def partner(array, axis, bit):
    return lax.ppermute(array, axis, [(i, i ^ 1 << bit) for i in range(lax.axis_size(axis))])


def slot_of(routes, experts):
    flat = routes.reshape(-1)
    owner = (flat[:, None] == jnp.arange(experts, dtype=jnp.int32)[None, :]).astype(jnp.int32)
    before = jnp.cumsum(owner, axis=0) - owner
    slot = jnp.sum(before * owner, axis=1)
    return (flat, slot)


def shards(tokens, cotangent, routes, gates, w_gate, w_up, w_down):
    tok_count = tokens.shape[0]
    groups = lax.axis_size("expert")
    experts = groups // SPLIT
    capacity = max(2, min(TOK_DEV, 5 * TOK_DEV * TOP // (4 * experts)))
    if groups == 8 and lax.axis_size("dp") == 4 and capacity % 16 == 0 and capacity > 64:
        return fused(capacity, tokens, cotangent, routes, gates, w_gate, w_up, w_down)
    piece = (capacity + SPLIT - 1) // SPLIT
    levels = SPLIT.bit_length() - 1
    here = lax.axis_index("expert")
    flat, slot = slot_of(routes, experts)
    pair_count = flat.shape[0]
    pair_tok = (
        (jnp.arange(pair_count, dtype=jnp.int32) // TOP)[:, None]
        == jnp.arange(tok_count, dtype=jnp.int32)[None, :]
    ).astype(jnp.bfloat16)
    rows_all = groups * piece
    row_ids = jnp.arange(rows_all, dtype=jnp.int32)
    dest = row_ids // piece
    row_expert = dest // SPLIT
    row_slot = dest % SPLIT + row_ids % piece * SPLIT
    placed = (flat[None, :] == row_expert[:, None]) & (slot[None, :] == row_slot[:, None])
    placed_f = placed.astype(jnp.float32)
    token_map = jnp.dot(
        placed.astype(jnp.bfloat16), pair_tok, preferred_element_type=jnp.float32
    ).astype(jnp.bfloat16)
    send_x = jnp.dot(token_map, tokens, preferred_element_type=jnp.float32).astype(jnp.bfloat16)
    send_dy = jnp.dot(token_map, cotangent, preferred_element_type=jnp.float32).astype(jnp.bfloat16)
    send_gate = jnp.dot(
        placed_f, gates.reshape(-1).astype(jnp.float32), precision=lax.Precision.HIGHEST
    ).astype(jnp.bfloat16)
    full_gate, full_up, full_down = (
        lax.all_gather(w_gate, "dp", axis=1, tiled=True),
        lax.all_gather(w_up, "dp", axis=1, tiled=True),
        lax.all_gather(w_down, "dp", axis=1, tiled=True),
    )
    cur_x, cur_dy, cur_g = (
        lax.all_to_all(send_x, "expert", split_axis=0, concat_axis=0, tiled=True),
        lax.all_to_all(send_dy, "expert", split_axis=0, concat_axis=0, tiled=True),
        lax.all_to_all(send_gate, "expert", split_axis=0, concat_axis=0, tiled=True),
    )
    for bit in range(levels):
        got = partner((cur_x, cur_dy, cur_g), "expert", bit)
        lower = here // (1 << bit) % 2 == 0
        cur_x = jnp.where(
            lower,
            jnp.concatenate([cur_x, got[0]], axis=0),
            jnp.concatenate([got[0], cur_x], axis=0),
        )
        cur_dy = jnp.where(
            lower,
            jnp.concatenate([cur_dy, got[1]], axis=0),
            jnp.concatenate([got[1], cur_dy], axis=0),
        )
        cur_g = jnp.where(
            lower,
            jnp.concatenate([cur_g, got[2]], axis=0),
            jnp.concatenate([got[2], cur_g], axis=0),
        )
    rows_x, rows_dy, recv_gate = (cur_x, cur_dy, cur_g)
    pre_a = lax.dot_general(
        rows_x, full_gate, (((1,), (1,)), ((), ())), preferred_element_type=jnp.float32
    )
    pre_b = lax.dot_general(
        rows_x, full_up, (((1,), (1,)), ((), ())), preferred_element_type=jnp.float32
    )
    sig = jax.nn.sigmoid(pre_a)
    silu = pre_a * sig
    hidden = (silu * pre_b).astype(jnp.bfloat16)
    weight = recv_gate.astype(jnp.float32)
    probe = lax.dot_general(
        rows_dy, full_down, (((1,), (1,)), ((), ())), preferred_element_type=jnp.float32
    )
    share = jnp.sum(hidden.astype(jnp.float32) * probe, axis=1)
    scaled = (weight[:, None] * rows_dy.astype(jnp.float32)).astype(jnp.bfloat16)
    d_b = (weight[:, None] * probe * silu).astype(jnp.bfloat16)
    part_up = lax.dot_general(
        d_b, rows_x, (((0,), (0,)), ((), ())), preferred_element_type=jnp.float32
    )
    part_down = lax.dot_general(
        hidden, scaled, (((0,), (0,)), ((), ())), preferred_element_type=jnp.float32
    )
    folded = share.reshape(SPLIT, rows_all)
    for bit in reversed(range(levels)):
        half = folded.shape[0] // 2
        lower_half = folded[:half]
        upper_half = folded[half:]
        lower = here // (1 << bit) % 2 == 0
        keep = jnp.where(lower, lower_half, upper_half)
        away = jnp.where(lower, upper_half, lower_half)
        folded = keep + partner(away, "expert", bit)
    summed = lax.all_to_all(
        folded.reshape(rows_all), "expert", split_axis=0, concat_axis=0, tiled=True
    )
    gate_grad = jnp.dot(placed_f.T, summed, precision=lax.Precision.HIGHEST)
    sum_up, sum_down = (
        lax.psum_scatter(
            part_up.astype(jnp.bfloat16), "dp", scatter_dimension=1, tiled=True
        ).astype(jnp.float32),
        lax.psum_scatter(
            part_down.astype(jnp.bfloat16), "dp", scatter_dimension=1, tiled=True
        ).astype(jnp.float32),
    )
    return (
        sum_up.astype(jnp.bfloat16),
        sum_down.astype(jnp.bfloat16),
        gate_grad.reshape(tok_count, TOP),
    )


def solution(mesh):
    in_specs = (
        P(("expert", "dp"), None),
        P(("expert", "dp"), None),
        P(("expert", "dp"), None),
        P(("expert", "dp"), None),
        P("expert", "dp"),
        P("expert", "dp"),
        P("expert", "dp"),
    )
    out_specs = (P("expert", "dp"), P("expert", "dp"), P(("expert", "dp"), None))
    return jax.shard_map(shards, mesh=mesh, in_specs=in_specs, out_specs=out_specs, check_vma=False)
```
